32 devices in a mesh: mat: 4 (over z), pts: 8 (over y, x, core).
Axes of the slice: x: 2, y: 2, z: 4, core: 2. Of those that a mesh axis runs over, the one named last changes fastest.
Arguments:
- basis_values: bfloat16 [128, 2048, 512], P(('mat', 'pts')), may hold values from -6 to 6
- tile_ids: int32 [128, 4], P(('mat', 'pts')), may hold values from 0 to 3, as said below
- density_matrix: bfloat16 [512, 512], P('mat'), may hold values from -0.01171875 to 0.01171875
- descriptors: bfloat16 [128, 2048, 64], P(('mat', 'pts')), may hold values from -6 to 6
- grid_weights: float32 [128, 2048], P(('mat', 'pts')), may hold values from 0.25 to 2
- centre_ids: int32 [128, 2048], P(('mat', 'pts')), may hold values from 0 to 127
- density_scale: float32 [64], replicated, may hold values from -4 to 4
- norm_gain: float32 [64], replicated, may hold values from 0.1 to 1.9
- w_first: bfloat16 [64, 256], replicated, may hold values from -0.75 to 0.75
- b_first: float32 [256], replicated, may hold values from -3 to 3
- w_second: bfloat16 [256, 256], replicated, may hold values from -0.375 to 0.375
- b_second: float32 [256], replicated, may hold values from -3 to 3
- w_third: bfloat16 [256, 64], replicated, may hold values from -0.375 to 0.375
- b_third: float32 [64], replicated, may hold values from -3 to 3
Outputs:
- potential_matrix: bfloat16 [512, 512], P('mat', 'pts')
- centre_features: bfloat16 [128, 64], P('pts')
The draws below stay inside these ranges and needn't reach their ends.
Inputs may be any that keep to these rules, and one draw needn't show every extreme that they name: `tile_ids`: the 4 tiles t of one batch have 4 different values of t.
All inputs are finite; a program needn't handle non-finite values.
Results may differ from the reference program's by a relative error of at most 0.0064.
Values may be sent and summed in bfloat16 or wider, within the bound.
A program may use at most 64 MiB of HBM per device.

```python
import math
import jax
import jax.numpy as jnp
from jax import lax

ORB = 512
TILE = 128
FEAT = 64
HID = 256
PTS = 2048
BATCHES = 128
KT = 4
TPD = 1
NBAS = 512
NT = 4
NCENT = 128


def draw_tile_ids(key, part):
    owner_total = NT // TPD
    leading, trailing = jax.random.split(jax.random.fold_in(key, 11))
    scores = jax.random.randint(leading, (BATCHES, owner_total), 0, 1 << 20) * owner_total + jnp.arange(owner_total, dtype=jnp.int32)[None, :]
    owners = jnp.argsort(scores, axis=1)[:, :KT].astype(jnp.int32)
    local_tiles = jax.random.randint(trailing, (BATCHES, KT), 0, TPD).astype(jnp.int32)
    return (owners * TPD + local_tiles).astype(jnp.int32)


def centre_lists(key):
    return jax.random.randint(jax.random.fold_in(key, 23), (BATCHES, PTS), 0, NCENT).astype(jnp.int32)


def draw_centre_ids(key, part):
    return centre_lists(key)


def draw_descriptors(key, part):
    owners = centre_lists(key)
    spread_key, value_key = jax.random.split(jax.random.fold_in(key, 29))
    log_scales = jax.random.uniform(spread_key, (NCENT, FEAT), jnp.float32, math.log(0.3), math.log(3.0))
    values = jax.random.normal(value_key, (BATCHES, PTS, FEAT), jnp.float32)
    scales = jnp.exp(log_scales)[owners]
    return jnp.clip(scales * values, -6.0, 6.0).astype(jnp.bfloat16)


def level_of(own_key, dims, shards, low, largest):
    loudness, own = 1.0, jax.random.fold_in(own_key, 6)
    for position, parts in shards:
        steps = jnp.exp(jax.random.uniform(jax.random.fold_in(own, position), (parts,), jnp.float32, low / len(shards), largest / len(shards)))
        loudness = loudness * jnp.repeat(steps, dims[position] // parts).reshape([-1 if axis == position else 1 for axis in range(len(dims))])
    return loudness


def scatter_about(rng, dims, width, most, pieces=(), kind=jnp.bfloat16):
    array = width * jax.random.normal(rng, dims, jnp.float32)
    if pieces:
        array = array * level_of(rng, dims, pieces, -0.22, 0.18)
    return jnp.clip(array, -most, most).astype(kind)


def setup_inputs(seed: int = 0) -> dict:
    arg_keys = jax.random.split(jax.random.key(seed), 15)
    basis_values = scatter_about(arg_keys[0], (BATCHES, PTS, ORB), 1.0, 6.0, ((0, 32),))
    tile_ids = draw_tile_ids(jax.random.fold_in(arg_keys[14], 71), 0)
    density_matrix = scatter_about(arg_keys[2], (NBAS, NBAS), (ORB * ORB) ** -0.5, 0.01171875, ((0, 4),))
    descriptors = draw_descriptors(jax.random.fold_in(arg_keys[14], 71), 0)
    grid_weights = jnp.clip(jnp.exp(math.log(2.0) - 2.0794415 * jax.random.uniform(arg_keys[4], (BATCHES, PTS), jnp.float32) ** level_of(arg_keys[4], (BATCHES, PTS), ((0, 32),), -0.2, 0.2)), 0.25, 2.0)
    centre_ids = draw_centre_ids(jax.random.fold_in(arg_keys[14], 71), 0)
    density_scale = scatter_about(arg_keys[6], (FEAT,), 1.0, 4.0, (), jnp.float32)
    norm_gain = jnp.clip(1.0 + 0.18 * jax.random.normal(arg_keys[7], (FEAT,), jnp.float32), 0.1, 1.9)
    w_first = scatter_about(arg_keys[8], (FEAT, HID), FEAT ** -0.5, 0.75)
    b_first = scatter_about(arg_keys[9], (HID,), 0.5, 3.0, (), jnp.float32)
    w_second = scatter_about(arg_keys[10], (HID, HID), HID ** -0.5, 0.375)
    b_second = scatter_about(arg_keys[11], (HID,), 0.5, 3.0, (), jnp.float32)
    w_third = scatter_about(arg_keys[12], (HID, FEAT), HID ** -0.5, 0.375)
    b_third = scatter_about(arg_keys[13], (FEAT,), 0.5, 3.0, (), jnp.float32)
    return {"basis_values": basis_values, "tile_ids": tile_ids, "density_matrix": density_matrix, "descriptors": descriptors, "grid_weights": grid_weights, "centre_ids": centre_ids, "density_scale": density_scale, "norm_gain": norm_gain, "w_first": w_first, "b_first": b_first, "w_second": w_second, "b_second": b_second, "w_third": w_third, "b_third": b_third}


def orbital_rows(tile_list):
    offsets = jnp.arange(TILE, dtype=jnp.int32)
    return (tile_list.astype(jnp.int32)[:, None] * TILE + offsets[None, :]).reshape(-1).astype(jnp.int32)

def centre_network(summed, norm_gain, w_first, b_first, w_second, b_second, w_third, b_third):
    inverse = lax.rsqrt(lax.optimization_barrier(jnp.mean(summed * summed, axis=1, keepdims=True)) + 1e-05)
    normed = (summed * inverse * norm_gain).astype(jnp.bfloat16)
    hidden_one = jax.nn.silu(jnp.dot(normed, w_first, preferred_element_type=jnp.float32) + b_first).astype(jnp.bfloat16)
    hidden_two = jax.nn.silu(jnp.dot(hidden_one, w_second, preferred_element_type=jnp.float32) + b_second).astype(jnp.bfloat16)
    return (jnp.dot(hidden_two, w_third, preferred_element_type=jnp.float32) + b_third).astype(jnp.bfloat16)

def reference(basis_values, tile_ids, density_matrix, descriptors, grid_weights, centre_ids, density_scale, norm_gain, w_first, b_first, w_second, b_second, w_third, b_third):

    def batch_density(inputs):
        values, tile_list = inputs
        orbital = orbital_rows(tile_list)
        panel_full = density_matrix[orbital][:, orbital]
        projected = jnp.dot(values, panel_full, preferred_element_type=jnp.float32)
        return lax.optimization_barrier(jnp.sum(values.astype(jnp.float32) * projected, axis=1))
    density = lax.map(batch_density, (basis_values, tile_ids))
    radial_terms = descriptors.astype(jnp.float32)
    features = jax.nn.silu(density[:, :, None] * density_scale + radial_terms)
    weighted_feat = grid_weights[:, :, None] * features
    centre_sum = jax.ops.segment_sum(weighted_feat.reshape(-1, FEAT), centre_ids.reshape(-1), num_segments=NCENT)
    centre_features = centre_network(centre_sum, norm_gain, w_first, b_first, w_second, b_second, w_third, b_third)
    nearest = centre_features[centre_ids].astype(jnp.float32)
    factor = NT / (KT * math.sqrt(PTS * FEAT * BATCHES))
    point_potential = grid_weights * density * lax.optimization_barrier(jnp.sum(nearest * radial_terms, axis=2)) * factor

    def assemble(accumulated, inputs):
        values, tile_list, local_potential = inputs
        orbital = orbital_rows(tile_list)
        weighted = (local_potential[:, None] * values.astype(jnp.float32)).astype(jnp.bfloat16)
        tile_block = jnp.dot(values.T, weighted, preferred_element_type=jnp.float32)
        return (accumulated.at[orbital[:, None], orbital[None, :]].add(tile_block), None)
    accumulated, ignored = lax.scan(assemble, jnp.zeros((NBAS, NBAS), jnp.float32), (basis_values, tile_ids, point_potential))
    return (accumulated.astype(jnp.bfloat16), centre_features)
```

```python
import functools
import math

import jax
import jax.numpy as jnp
from jax import lax
from jax.experimental import pallas as pl
from jax.experimental.pallas import tpu as pltpu
from jax.sharding import PartitionSpec as P

CHUNK = 512
SPLIT = 2
MESH = pl.DeviceIdType.MESH
F32 = jnp.float32
BF16 = jnp.bfloat16
NT_DIMS = (((1,), (1,)), ((), ()))


def silu(v):
    h = 0.5 * v
    return h + h * jnp.tanh(h)


def kernel(
    nm, npts, factor,
    v_hbm, d_hbm, tiles, dm, gw, ids, scale, gain, w1, b1, w2, b2, w3, b3,
    out_pot, out_cf,
    vbuf, dbuf, vt, dt, oh, gws, dens, pps, panel, cpart, cs_src, cs_in, cz_src, cz_in,
    full, cf_s, cft, acc, snd, rin, red, zsnd, zin,
    vsem, dsem, ag_s, ag_r, fw_s, fw_r, cs_s, cs_r, cz_s, cz_r, cg_s, cg_r, rp_s, rp_r, rz_s, rz_r,
):
    m = lax.axis_index("mat")
    p = lax.axis_index("pts")
    batches, points, orbitals = vbuf.shape
    per_batch = tiles.shape[1]
    tile = orbitals // per_batch
    rows, nb = dm.shape
    ntile = nb // tile
    feat = dbuf.shape[1]
    ncent = oh.shape[1]
    per = points // CHUNK
    chunks = batches * per
    slab = nb // npts
    piece = rows // SPLIT

    for b in range(batches):
        pltpu.make_async_copy(v_hbm.at[b], vbuf.at[b], vsem.at[b]).start()
        pltpu.make_async_copy(d_hbm.at[b], dbuf.at[b], dsem.at[b]).start()

    barrier = pltpu.get_barrier_semaphore()
    for k in range(1, npts):
        pl.semaphore_signal(barrier, inc=1, device_id={"pts": lax.rem(p + k, npts)}, device_id_type=MESH)
    for k in range(1, nm):
        pl.semaphore_signal(barrier, inc=1, device_id={"mat": lax.rem(m + k, nm)}, device_id_type=MESH)
    pl.semaphore_wait(barrier, npts + nm - 2)

    def remote(src, dst, s, r, **where):
        return pltpu.make_async_remote_copy(
            src_ref=src, dst_ref=dst, send_sem=s, recv_sem=r, device_id=where, device_id_type=MESH
        )

    def at_rows(owner, part):
        return pl.ds(pl.multiple_of(owner * rows + part * piece, piece), piece)

    g = lax.rem(p, SPLIT)
    base = p - g
    ag = []
    for k in range(1, nm):
        ag.append(remote(
            dm.at[pl.ds(pl.multiple_of(g * piece, piece), piece)], panel.at[at_rows(m, g)],
            ag_s.at[k - 1], ag_r.at[k - 1], mat=lax.rem(m + k, nm)))
    for c in ag:
        c.start()
    panel[pl.ds(pl.multiple_of(m * rows, rows), rows), :] = dm[...]

    def prepare(b):
        pltpu.make_async_copy(v_hbm.at[b], vbuf.at[b], vsem.at[b]).wait()
        pltpu.make_async_copy(d_hbm.at[b], dbuf.at[b], dsem.at[b]).wait()
        held = [tiles[b, j] for j in range(per_batch)]

        def body(i, carry):
            ch = b * per + i
            r0 = pl.multiple_of(i * CHUNK, CHUNK)
            for t in range(ntile):
                x = vbuf[b, pl.ds(r0, CHUNK), 0:tile]
                if ntile != per_batch:
                    x = jnp.where(held[0] == t, x, jnp.zeros_like(x))
                for j in range(1, per_batch):
                    x = jnp.where(held[j] == t, vbuf[b, pl.ds(r0, CHUNK), j * tile:(j + 1) * tile], x)
                x = x.T
                vt[ch, t * tile:(t + 1) * tile, :] = x
            dt[ch] = dbuf[b, :, pl.ds(r0, CHUNK)]
            row = ids[b:b + 1, pl.ds(r0, CHUNK)]
            which = lax.broadcasted_iota(jnp.int32, (ncent, CHUNK), 0)
            oh[ch] = jnp.where(which == row, 1.0, 0.0).astype(BF16)
            gws[ch] = gw[b:b + 1, pl.ds(r0, CHUNK)]
            return carry

        lax.fori_loop(0, per, body, 0)

    fw = []
    for b in range(batches):
        prepare(b)
        if b == min(1, batches - 1):
            for k in range(1, nm):
                ag[k - 1].wait_recv()
                held = panel.at[at_rows(lax.rem(m - k + nm, nm), g)]
                for s in range(1, SPLIT):
                    i = (k - 1) * (SPLIT - 1) + s - 1
                    c = remote(held, held, fw_s.at[i], fw_r.at[i], pts=base + lax.rem(g + s, SPLIT))
                    c.start()
                    fw.append(c)
    for c in fw:
        c.wait_recv()

    scale_col = jnp.broadcast_to(scale[...], (128, feat)).T[:, :1]
    cpart[...] = jnp.zeros_like(cpart)

    def density_step(ch, carry):
        x = vt[ch]
        q = jnp.dot(panel[...], x, preferred_element_type=F32)
        d = jnp.sum(q * x.astype(F32), axis=0, keepdims=True)
        dens[ch] = d
        wf = gws[ch] * silu(d * scale_col + dt[ch].astype(F32))
        high = wf.astype(BF16)
        low = (wf - high.astype(F32)).astype(BF16)
        both = lax.dot_general(
            jnp.concatenate([high, low], axis=0), oh[ch], NT_DIMS, preferred_element_type=F32)
        cpart[...] += both[:feat] + both[feat:]
        return carry

    lax.fori_loop(0, chunks, density_step, 0)

    fp = feat // npts
    for i in range(npts):
        cs_src[i] = cpart[i * fp:(i + 1) * fp, :]
    cs = []
    for k in range(1, npts):
        to = lax.rem(p + k, npts)
        c = remote(cs_src.at[to], cs_in.at[k - 1], cs_s.at[k - 1], cs_r.at[k - 1], pts=to)
        c.start()
        cs.append(c)
    mine = cs_src[p]
    for k in range(1, npts):
        cs[k - 1].wait_recv()
        mine = mine + cs_in[k - 1]
    cz_src[...] = mine
    cz = []
    for k in range(1, nm):
        c = remote(cz_src, cz_in.at[m], cz_s.at[k - 1], cz_r.at[k - 1], mat=lax.rem(m + k, nm))
        c.start()
        cz.append(c)
    cz_in[m] = mine
    for c in cz:
        c.wait_recv()
    total = cz_in[0]
    for i in range(1, nm):
        total = total + cz_in[i]
    full[p] = total
    cg = []
    for k in range(1, npts):
        c = remote(full.at[p], full.at[p], cg_s.at[k - 1], cg_r.at[k - 1], pts=lax.rem(p + k, npts))
        c.start()
        cg.append(c)
    for c in cg:
        c.wait_recv()

    summed = jnp.concatenate([full[i] for i in range(npts)], axis=0).T
    inverse = lax.rsqrt(jnp.mean(summed * summed, axis=1, keepdims=True) + 1e-05)
    normed = (summed * inverse * gain[...]).astype(BF16)
    one = silu(jnp.dot(normed, w1[...], preferred_element_type=F32) + b1[...]).astype(BF16)
    two = silu(jnp.dot(one, w2[...], preferred_element_type=F32) + b2[...]).astype(BF16)
    cf = (lax.dot_general(two, w3[...], NT_DIMS, preferred_element_type=F32) + b3[...]).astype(BF16).astype(F32)
    cf_s[...] = cf
    cft[...] = cf.T.astype(BF16)
    cent = out_cf.shape[0]
    out_cf[...] = cf_s[pl.ds(pl.multiple_of(p * cent, cent), cent), :].astype(BF16)

    half = nb // 2
    hp = npts // 2
    acc[...] = jnp.zeros_like(acc)
    rp = []
    for h in range(2):
        def block_step(ch, carry):
            if h == 0:
                near = jnp.dot(cft[...], oh[ch], preferred_element_type=F32)
                along = jnp.sum(near * dt[ch].astype(F32), axis=0, keepdims=True)
                pp = gws[ch] * dens[ch] * along * factor
                pps[ch] = pp
            else:
                pp = pps[ch]
            w = (vt[ch, h * half:(h + 1) * half, :].astype(F32) * pp).astype(BF16)
            r = lax.dot_general(w, vt[ch], NT_DIMS, preferred_element_type=F32)
            acc[h * hp:(h + 1) * hp] += r.reshape(hp, slab, nb)
            return carry

        lax.fori_loop(0, chunks, block_step, 0)
        for i in range(h * hp, (h + 1) * hp):
            snd[i] = acc[i].astype(BF16)
        for k in list(range(1, hp)) + [0]:
            to = h * hp + lax.rem(p + k, hp)
            c = remote(snd.at[to], rin.at[p], rp_s.at[to], rp_r.at[p], pts=to)
            rp.append((to, c))

            @pl.when(to != p)
            def _():
                c.start()

    mine = acc[p]
    for k in range(1, npts):
        src = lax.rem(p + k, npts)
        remote(snd.at[src], rin.at[src], rp_s.at[src], rp_r.at[src], pts=src).wait_recv()
        mine = mine + rin[src].astype(F32)
    width = nb // nm
    for j in range(nm):
        red[j] = mine[:, j * width:(j + 1) * width]
        zsnd[j] = mine[:, j * width:(j + 1) * width].astype(BF16)
    rz = []
    for k in range(1, nm):
        to = lax.rem(m + k, nm)
        c = remote(zsnd.at[to], zin.at[k - 1], rz_s.at[k - 1], rz_r.at[k - 1], mat=to)
        c.start()
        rz.append(c)
    mine = red[m]
    for k in range(1, nm):
        rz[k - 1].wait_recv()
        mine = mine + zin[k - 1].astype(F32)
    out_pot[...] = mine.astype(BF16)

    for c in ag + fw + cs + cz + cg + rz:
        c.wait_send()
    for to, c in rp:
        @pl.when(to != p)
        def _():
            c.wait_send()


def shards(
    nm, npts,
    basis_values, tile_ids, density_matrix, descriptors, grid_weights, centre_ids,
    density_scale, norm_gain, w_first, b_first, w_second, b_second, w_third, b_third,
):
    batches, points, orbitals = basis_values.shape
    per_batch = tile_ids.shape[1]
    tile = orbitals // per_batch
    rows, nb = density_matrix.shape
    feat = descriptors.shape[2]
    ntile = nb // tile
    cent = 16
    ncent = cent * npts
    chunks = batches * points // CHUNK
    slab = nb // npts
    width = nb // nm
    factor = ntile / (per_batch * math.sqrt(points * feat * batches * nm * npts))
    vm = pl.BlockSpec(memory_space=pltpu.VMEM)
    anyw = pl.BlockSpec(memory_space=pl.ANY)
    fp = feat // npts
    dma = pltpu.SemaphoreType.DMA
    nfw = (nm - 1) * (SPLIT - 1)
    potential, centre_features = pl.pallas_call(
        functools.partial(kernel, nm, npts, factor),
        out_shape=(
            jax.ShapeDtypeStruct((slab, width), BF16),
            jax.ShapeDtypeStruct((cent, feat), BF16),
        ),
        in_specs=[anyw, anyw, pl.BlockSpec(memory_space=pltpu.SMEM)] + [vm] * 11,
        out_specs=(vm, vm),
        scratch_shapes=[
            pltpu.VMEM((batches, points, orbitals), BF16),
            pltpu.VMEM((batches, feat, points), BF16),
            pltpu.VMEM((chunks, nb, CHUNK), BF16),
            pltpu.VMEM((chunks, feat, CHUNK), BF16),
            pltpu.VMEM((chunks, ncent, CHUNK), BF16),
            pltpu.VMEM((chunks, 1, CHUNK), F32),
            pltpu.VMEM((chunks, 1, CHUNK), F32),
            pltpu.VMEM((chunks, 1, CHUNK), F32),
            pltpu.VMEM((nb, nb), BF16),
            pltpu.VMEM((feat, ncent), F32),
            pltpu.VMEM((npts, fp, ncent), F32),
            pltpu.VMEM((npts, fp, ncent), F32),
            pltpu.VMEM((fp, ncent), F32),
            pltpu.VMEM((nm, fp, ncent), F32),
            pltpu.VMEM((npts, fp, ncent), F32),
            pltpu.VMEM((ncent, feat), F32),
            pltpu.VMEM((feat, ncent), BF16),
            pltpu.VMEM((npts, slab, nb), F32),
            pltpu.VMEM((npts, slab, nb), BF16),
            pltpu.VMEM((npts, slab, nb), BF16),
            pltpu.VMEM((nm, slab, width), F32),
            pltpu.VMEM((nm, slab, width), BF16),
            pltpu.VMEM((nm, slab, width), BF16),
            dma((batches,)), dma((batches,)),
            dma((nm - 1,)), dma((nm - 1,)),
            dma((nfw,)), dma((nfw,)),
            dma((npts - 1,)), dma((npts - 1,)),
            dma((nm - 1,)), dma((nm - 1,)),
            dma((npts - 1,)), dma((npts - 1,)),
            dma((npts,)), dma((npts,)),
            dma((nm - 1,)), dma((nm - 1,)),
        ],
        compiler_params=pltpu.CompilerParams(
            collective_id=0, has_side_effects=True, vmem_limit_bytes=60 * 1024 * 1024
        ),
    )(
        basis_values, descriptors.transpose(0, 2, 1), tile_ids, density_matrix, grid_weights, centre_ids,
        density_scale.reshape(1, -1), norm_gain.reshape(1, -1),
        w_first, b_first.reshape(1, -1), w_second, b_second.reshape(1, -1),
        w_third.T, b_third.reshape(1, -1),
    )
    return (potential.T, centre_features)


def solution(mesh):
    return jax.shard_map(
        functools.partial(shards, mesh.shape["mat"], mesh.shape["pts"]),
        mesh=mesh,
        in_specs=(
            P(("mat", "pts"), None, None),
            P(("mat", "pts"), None),
            P("mat", None),
            P(("mat", "pts"), None, None),
            P(("mat", "pts"), None),
            P(("mat", "pts"), None),
            P(), P(), P(), P(), P(), P(), P(), P(),
        ),
        out_specs=(P("mat", "pts"), P("pts", None)),
        check_vma=False,
    )
```

```python
import functools
import math

import jax
import jax.numpy as jnp
from jax import lax
from jax.experimental import pallas as pl
from jax.experimental.pallas import tpu as pltpu
from jax.sharding import PartitionSpec as P

CHUNK = 512
SPLIT = 2
MESH = pl.DeviceIdType.MESH
F32 = jnp.float32
BF16 = jnp.bfloat16
NT_DIMS = (((1,), (1,)), ((), ()))


def silu(v):
    h = 0.5 * v
    return h + h * jnp.tanh(h)


def place(pot, cf, out_pot, out_cf):
    out_pot[...] = pot[...]
    out_cf[...] = cf[...]


def kernel(
    nm, npts, factor,
    v_hbm, d_hbm, tiles, dm, gw, ids, scale, gain, w1, b1, w2, b2, w3, b3,
    out_pot, out_cf,
    vbuf, dbuf, vt, dt, oh, gws, dens, pps, panel, cpart, cs_src, cs_in, cz_src, cz_in,
    full, cf_s, cft, acc, snd, rin, red, zsnd, zin,
    vsem, dsem, ag_s, ag_r, fw_s, fw_r, cs_s, cs_r, cz_s, cz_r, cg_s, cg_r, rp_s, rp_r, rz_s, rz_r,
):
    m = lax.axis_index("mat")
    p = lax.axis_index("pts")
    batches, points, orbitals = vbuf.shape
    per_batch = tiles.shape[1]
    tile = orbitals // per_batch
    rows, nb = dm.shape
    ntile = nb // tile
    feat = dbuf.shape[1]
    ncent = oh.shape[1]
    per = points // CHUNK
    chunks = batches * per
    slab = nb // npts
    piece = rows // SPLIT

    for b in range(batches):
        pltpu.make_async_copy(v_hbm.at[b], vbuf.at[b], vsem.at[b]).start()
        pltpu.make_async_copy(d_hbm.at[b], dbuf.at[b], dsem.at[b]).start()

    barrier = pltpu.get_barrier_semaphore()
    for k in range(1, npts):
        pl.semaphore_signal(barrier, inc=1, device_id={"pts": lax.rem(p + k, npts)}, device_id_type=MESH)
    for k in range(1, nm):
        pl.semaphore_signal(barrier, inc=1, device_id={"mat": lax.rem(m + k, nm)}, device_id_type=MESH)
    pl.semaphore_wait(barrier, npts + nm - 2)

    def remote(src, dst, s, r, **where):
        return pltpu.make_async_remote_copy(
            src_ref=src, dst_ref=dst, send_sem=s, recv_sem=r, device_id=where, device_id_type=MESH
        )

    def at_rows(owner, part):
        return pl.ds(pl.multiple_of(owner * rows + part * piece, piece), piece)

    g = lax.rem(p, SPLIT)
    base = p - g
    ag = []
    for k in range(1, nm):
        ag.append(remote(
            dm.at[pl.ds(pl.multiple_of(g * piece, piece), piece)], panel.at[at_rows(m, g)],
            ag_s.at[k - 1], ag_r.at[k - 1], mat=lax.rem(m + k, nm)))
    for c in ag:
        c.start()
    panel[pl.ds(pl.multiple_of(m * rows, rows), rows), :] = dm[...]

    def prepare(b):
        pltpu.make_async_copy(v_hbm.at[b], vbuf.at[b], vsem.at[b]).wait()
        pltpu.make_async_copy(d_hbm.at[b], dbuf.at[b], dsem.at[b]).wait()
        held = [tiles[b, j] for j in range(per_batch)]

        def body(i, carry):
            ch = b * per + i
            r0 = pl.multiple_of(i * CHUNK, CHUNK)
            for t in range(ntile):
                x = vbuf[b, pl.ds(r0, CHUNK), 0:tile]
                if ntile != per_batch:
                    x = jnp.where(held[0] == t, x, jnp.zeros_like(x))
                for j in range(1, per_batch):
                    x = jnp.where(held[j] == t, vbuf[b, pl.ds(r0, CHUNK), j * tile:(j + 1) * tile], x)
                x = x.T
                vt[ch, t * tile:(t + 1) * tile, :] = x
            dt[ch] = dbuf[b, :, pl.ds(r0, CHUNK)]
            row = ids[b:b + 1, pl.ds(r0, CHUNK)]
            which = lax.broadcasted_iota(jnp.int32, (ncent, CHUNK), 0)
            oh[ch] = jnp.where(which == row, 1.0, 0.0).astype(BF16)
            gws[ch] = gw[b:b + 1, pl.ds(r0, CHUNK)]
            return carry

        lax.fori_loop(0, per, body, 0)

    fw = []
    for b in range(batches):
        prepare(b)
        if b == min(1, batches - 1):
            for k in range(1, nm):
                ag[k - 1].wait_recv()
                held = panel.at[at_rows(lax.rem(m - k + nm, nm), g)]
                for s in range(1, SPLIT):
                    i = (k - 1) * (SPLIT - 1) + s - 1
                    c = remote(held, held, fw_s.at[i], fw_r.at[i], pts=base + lax.rem(g + s, SPLIT))
                    c.start()
                    fw.append(c)
    for c in fw:
        c.wait_recv()

    scale_col = jnp.broadcast_to(scale[...], (128, feat)).T[:, :1]
    cpart[...] = jnp.zeros_like(cpart)

    def density_step(ch, carry):
        x = vt[ch]
        q = jnp.dot(panel[...], x, preferred_element_type=F32)
        d = jnp.sum(q * x.astype(F32), axis=0, keepdims=True)
        dens[ch] = d
        wf = gws[ch] * silu(d * scale_col + dt[ch].astype(F32))
        high = wf.astype(BF16)
        low = (wf - high.astype(F32)).astype(BF16)
        both = lax.dot_general(
            jnp.concatenate([high, low], axis=0), oh[ch], NT_DIMS, preferred_element_type=F32)
        cpart[...] += both[:feat] + both[feat:]
        return carry

    lax.fori_loop(0, chunks, density_step, 0)

    fp = feat // npts
    for i in range(npts):
        cs_src[i] = cpart[i * fp:(i + 1) * fp, :]
    cs = []
    for k in range(1, npts):
        to = lax.rem(p + k, npts)
        c = remote(cs_src.at[to], cs_in.at[k - 1], cs_s.at[k - 1], cs_r.at[k - 1], pts=to)
        c.start()
        cs.append(c)
    mine = cs_src[p]
    for k in range(1, npts):
        cs[k - 1].wait_recv()
        mine = mine + cs_in[k - 1]
    cz_src[...] = mine
    cz = []
    for k in range(1, nm):
        c = remote(cz_src, cz_in.at[m], cz_s.at[k - 1], cz_r.at[k - 1], mat=lax.rem(m + k, nm))
        c.start()
        cz.append(c)
    cz_in[m] = mine
    for c in cz:
        c.wait_recv()
    total = cz_in[0]
    for i in range(1, nm):
        total = total + cz_in[i]
    full[p] = total
    cg = []
    for k in range(1, npts):
        c = remote(full.at[p], full.at[p], cg_s.at[k - 1], cg_r.at[k - 1], pts=lax.rem(p + k, npts))
        c.start()
        cg.append(c)
    for c in cg:
        c.wait_recv()

    summed = jnp.concatenate([full[i] for i in range(npts)], axis=0).T
    inverse = lax.rsqrt(jnp.mean(summed * summed, axis=1, keepdims=True) + 1e-05)
    normed = (summed * inverse * gain[...]).astype(BF16)
    one = silu(jnp.dot(normed, w1[...], preferred_element_type=F32) + b1[...]).astype(BF16)
    two = silu(jnp.dot(one, w2[...], preferred_element_type=F32) + b2[...]).astype(BF16)
    cf = (lax.dot_general(two, w3[...], NT_DIMS, preferred_element_type=F32) + b3[...]).astype(BF16).astype(F32)
    cf_s[...] = cf
    cft[...] = cf.T.astype(BF16)
    cent = out_cf.shape[0]
    out_cf[...] = cf_s[pl.ds(pl.multiple_of(p * cent, cent), cent), :].astype(BF16)

    half = nb // 2
    hp = npts // 2
    acc[...] = jnp.zeros_like(acc)
    rp = []
    for h in range(2):
        def block_step(ch, carry):
            if h == 0:
                near = jnp.dot(cft[...], oh[ch], preferred_element_type=F32)
                along = jnp.sum(near * dt[ch].astype(F32), axis=0, keepdims=True)
                pp = gws[ch] * dens[ch] * along * factor
                pps[ch] = pp
            else:
                pp = pps[ch]
            w = (vt[ch, h * half:(h + 1) * half, :].astype(F32) * pp).astype(BF16)
            right = vt[ch] if h == 0 else vt[ch, half:, :]
            r = lax.dot_general(w, right, NT_DIMS, preferred_element_type=F32)
            acc[h * hp:(h + 1) * hp, :, h * half:] += r.reshape(hp, slab, nb - h * half)
            return carry

        if h == 1:
            corner = acc[:hp, :, half:].reshape(half, half)
            acc[hp:, :, :half] = corner.T.reshape(hp, slab, half)
        lax.fori_loop(0, chunks, block_step, 0)
        for i in range(h * hp, (h + 1) * hp):
            snd[i] = acc[i].astype(BF16)
        for k in list(range(1, hp)) + [0]:
            to = h * hp + lax.rem(p + k, hp)
            c = remote(snd.at[to], rin.at[p], rp_s.at[to], rp_r.at[p], pts=to)
            rp.append((to, c))

            @pl.when(to != p)
            def _():
                c.start()

    mine = acc[p]
    for k in range(1, npts):
        src = lax.rem(p + k, npts)
        remote(snd.at[src], rin.at[src], rp_s.at[src], rp_r.at[src], pts=src).wait_recv()
        mine = mine + rin[src].astype(F32)
    width = nb // nm
    for j in range(nm):
        red[j] = mine[:, j * width:(j + 1) * width]
        zsnd[j] = mine[:, j * width:(j + 1) * width].astype(BF16)
    rz = []
    for k in range(1, nm):
        to = lax.rem(m + k, nm)
        c = remote(zsnd.at[to], zin.at[k - 1], rz_s.at[k - 1], rz_r.at[k - 1], mat=to)
        c.start()
        rz.append(c)
    mine = red[m]
    for k in range(1, nm):
        rz[k - 1].wait_recv()
        mine = mine + zin[k - 1].astype(F32)
    out_pot[...] = mine.astype(BF16)

    for c in ag + fw + cs + cz + cg + rz:
        c.wait_send()
    for to, c in rp:
        @pl.when(to != p)
        def _():
            c.wait_send()


def shards(
    nm, npts,
    basis_values, tile_ids, density_matrix, descriptors, grid_weights, centre_ids,
    density_scale, norm_gain, w_first, b_first, w_second, b_second, w_third, b_third,
):
    batches, points, orbitals = basis_values.shape
    per_batch = tile_ids.shape[1]
    tile = orbitals // per_batch
    rows, nb = density_matrix.shape
    feat = descriptors.shape[2]
    ntile = nb // tile
    cent = 16
    ncent = cent * npts
    chunks = batches * points // CHUNK
    slab = nb // npts
    width = nb // nm
    factor = ntile / (per_batch * math.sqrt(points * feat * batches * nm * npts))
    vm = pl.BlockSpec(memory_space=pltpu.VMEM)
    anyw = pl.BlockSpec(memory_space=pl.ANY)
    fp = feat // npts
    dma = pltpu.SemaphoreType.DMA
    nfw = (nm - 1) * (SPLIT - 1)
    potential, centre_features = pl.pallas_call(
        functools.partial(kernel, nm, npts, factor),
        out_shape=(
            jax.ShapeDtypeStruct((slab, width), BF16),
            jax.ShapeDtypeStruct((cent, feat), BF16),
        ),
        in_specs=[anyw, anyw, pl.BlockSpec(memory_space=pltpu.SMEM)] + [vm] * 11,
        out_specs=(vm, vm),
        scratch_shapes=[
            pltpu.VMEM((batches, points, orbitals), BF16),
            pltpu.VMEM((batches, feat, points), BF16),
            pltpu.VMEM((chunks, nb, CHUNK), BF16),
            pltpu.VMEM((chunks, feat, CHUNK), BF16),
            pltpu.VMEM((chunks, ncent, CHUNK), BF16),
            pltpu.VMEM((chunks, 1, CHUNK), F32),
            pltpu.VMEM((chunks, 1, CHUNK), F32),
            pltpu.VMEM((chunks, 1, CHUNK), F32),
            pltpu.VMEM((nb, nb), BF16),
            pltpu.VMEM((feat, ncent), F32),
            pltpu.VMEM((npts, fp, ncent), F32),
            pltpu.VMEM((npts, fp, ncent), F32),
            pltpu.VMEM((fp, ncent), F32),
            pltpu.VMEM((nm, fp, ncent), F32),
            pltpu.VMEM((npts, fp, ncent), F32),
            pltpu.VMEM((ncent, feat), F32),
            pltpu.VMEM((feat, ncent), BF16),
            pltpu.VMEM((npts, slab, nb), F32),
            pltpu.VMEM((npts, slab, nb), BF16),
            pltpu.VMEM((npts, slab, nb), BF16),
            pltpu.VMEM((nm, slab, width), F32),
            pltpu.VMEM((nm, slab, width), BF16),
            pltpu.VMEM((nm, slab, width), BF16),
            dma((batches,)), dma((batches,)),
            dma((nm - 1,)), dma((nm - 1,)),
            dma((nfw,)), dma((nfw,)),
            dma((npts - 1,)), dma((npts - 1,)),
            dma((nm - 1,)), dma((nm - 1,)),
            dma((npts - 1,)), dma((npts - 1,)),
            dma((npts,)), dma((npts,)),
            dma((nm - 1,)), dma((nm - 1,)),
        ],
        compiler_params=pltpu.CompilerParams(
            collective_id=0, has_side_effects=True, vmem_limit_bytes=60 * 1024 * 1024
        ),
    )(
        basis_values, descriptors.transpose(0, 2, 1), tile_ids, density_matrix, grid_weights, centre_ids,
        density_scale.reshape(1, -1), norm_gain.reshape(1, -1),
        w_first, b_first.reshape(1, -1), w_second, b_second.reshape(1, -1),
        w_third.T, b_third.reshape(1, -1),
    )
    potential, centre_features = pl.pallas_call(
        place,
        out_shape=(
            jax.ShapeDtypeStruct((slab, width), BF16),
            jax.ShapeDtypeStruct((cent, feat), BF16),
        ),
        in_specs=[vm, vm],
        out_specs=(vm, vm),
    )(potential, centre_features)
    return (potential.T, centre_features)


def solution(mesh):
    return jax.shard_map(
        functools.partial(shards, mesh.shape["mat"], mesh.shape["pts"]),
        mesh=mesh,
        in_specs=(
            P(("mat", "pts"), None, None),
            P(("mat", "pts"), None),
            P("mat", None),
            P(("mat", "pts"), None, None),
            P(("mat", "pts"), None),
            P(("mat", "pts"), None),
            P(), P(), P(), P(), P(), P(), P(), P(),
        ),
        out_specs=(P("mat", "pts"), P("pts", None)),
        check_vma=False,
    )
```
